128 devices in a mesh: seq: 32 (over x, y, core), trk: 4 (over z).
Axes of the slice: x: 4, y: 4, z: 4, core: 2. Of those that a mesh axis runs over, the one named last changes fastest.
Arguments:
- inputs: bfloat16 [4, 8192, 1536], P('trk', 'seq'), may hold values from -6 to 6
- first_depthwise_taps: float32 [3, 1536], replicated, may hold values from -3.5 to 3.5
- second_depthwise_taps: float32 [3, 1536], replicated, may hold values from -3.5 to 3.5
- first_pointwise_matrix: bfloat16 [1536, 1536], replicated, may hold values from -0.15625 to 0.15625
- second_pointwise_matrix: bfloat16 [1536, 1536], replicated, may hold values from -0.15625 to 0.15625
- head_weight: bfloat16 [1536, 7168], P(None, 'trk'), may hold values from -0.3125 to 0.3125
- pred_cotangent: bfloat16 [4, 3072, 7168], P(None, 'seq', 'trk'), may hold values from -1.1953125 to 1.1953125
- trunk_cotangent: bfloat16 [4, 8192, 1536], P('trk', 'seq'), may hold values from -3 to 3
Outputs:
- prediction: bfloat16 [4, 3072, 7168], P(None, 'seq', 'trk')
- trunk_output: bfloat16 [4, 8192, 1536], P('trk', 'seq')
- input_gradient_rows: float32 [4, 8192, 1536], P('trk', 'seq')
- grad_head: float32 [1536, 7168], P('seq', 'trk')
The draws below stay inside these ranges and needn't reach their ends.
All inputs are finite; a program needn't handle non-finite values.
Results may differ from the reference program's by a relative error of at most 0.015.
Values may be sent and summed in bfloat16 or wider, within the bound.
No kernel may reach another device: no remote copies, remote signals or barrier semaphores. Data moves between devices by JAX's collectives and lax.ppermute only.
A program may use at most 128 MiB of HBM per device.

```python
import jax
import jax.numpy as jnp
from jax import lax

D = 1536
TRACKS = 7168
DILATION_FIRST = 4
DILATION_SECOND = 8
BATCH = 4
BINS = 8192
CROP = 3072
START = 2560


def block_scale(own_key, extent, split, low, top_value):
    def one(axis_at, shards_of):
        heights = jax.random.uniform(jax.random.fold_in(jax.random.fold_in(own_key, 6), axis_at), (shards_of,), jnp.float32, low / len(split), top_value / len(split))
        return jnp.repeat(jnp.exp(heights), extent[axis_at] // shards_of).reshape((-1,) + (1,) * (len(extent) - axis_at - 1))

    factor_of = one(*split[0])
    for cut in split[1:]:
        factor_of = factor_of * one(*cut)
    return factor_of


def scatter_about(rng, dims, width, limit, shards=(), held_as=jnp.bfloat16):
    drawn = jax.random.normal(rng, dims, jnp.float32) * width
    if len(shards) > 0:
        drawn = block_scale(rng, dims, shards, -0.22, 0.18) * drawn
    return jnp.clip(drawn, min=-limit, max=limit).astype(held_as)


def setup_inputs(seed: int = 0) -> dict:
    arg_keys = jax.random.split(jax.random.key(seed), 9)
    return {
        "inputs": scatter_about(arg_keys[0], (BATCH, BINS, D), 1.0, 6.0, ((0, 4), (1, 32))),
        "first_depthwise_taps": scatter_about(arg_keys[1], (3, D), 3 ** -0.5, 3.5, (), jnp.float32),
        "second_depthwise_taps": scatter_about(arg_keys[2], (3, D), 3 ** -0.5, 3.5, (), jnp.float32),
        "first_pointwise_matrix": scatter_about(arg_keys[3], (D, D), D ** -0.5, 0.15625),
        "second_pointwise_matrix": scatter_about(arg_keys[4], (D, D), D ** -0.5, 0.15625),
        "head_weight": scatter_about(arg_keys[5], (D, TRACKS), (D // 4) ** -0.5, 0.3125, ((1, 4),)),
        "pred_cotangent": scatter_about(arg_keys[6], (BATCH, CROP, TRACKS), 0.2, 1.1953125, ((1, 32), (2, 4))),
        "trunk_cotangent": scatter_about(arg_keys[7], (BATCH, BINS, D), 0.5, 3.0, ((0, 4), (1, 32))),
    }


epsilon = 1e-06

def norm_gelu(values):
    scaled = values * lax.rsqrt(lax.optimization_barrier(jnp.mean(values * values, axis=-1, keepdims=True)) + epsilon)
    return jax.nn.gelu(scaled)

def rounded_length(values):
    return lax.optimization_barrier(values.astype(jnp.bfloat16))

def dilated_convolve(values, weights, dilation):
    length = values.shape[1]
    padded = jnp.pad(values, ((0, 0), (dilation, dilation), (0, 0)))
    return weights[0] * padded[:, :length] + weights[1] * values + weights[2] * padded[:, 2 * dilation:]

def product(inputs, matrix):
    flattened = inputs.reshape(-1, inputs.shape[-1])
    result = jnp.dot(flattened, matrix, preferred_element_type=jnp.float32)
    return result.reshape(inputs.shape[:-1] + (matrix.shape[1],))

def product_back(inputs, matrix):
    flattened = inputs.reshape(-1, inputs.shape[-1])
    result = jnp.dot(flattened, matrix.T, preferred_element_type=jnp.float32)
    return result.reshape(inputs.shape[:-1] + (matrix.shape[0],))

def residual_block_forward(inputs, depth, point, dilation):
    values = inputs.astype(jnp.float32)
    activation_value, backward = jax.vjp(norm_gelu, values)
    conv_out = dilated_convolve(rounded_length(activation_value).astype(jnp.float32), depth, dilation).astype(jnp.bfloat16)
    output = (values + product(conv_out, point)).astype(jnp.bfloat16)
    return (output, backward)

def residual_block_backward(grad_out, depth, point, dilation, backward):
    convolved_gradient = product_back(grad_out, point).astype(jnp.bfloat16)
    activation_gradient = dilated_convolve(convolved_gradient.astype(jnp.float32), depth[::-1], dilation)
    return grad_out.astype(jnp.float32) + backward(activation_gradient)[0]

def orient(values):
    reverse_strand = jnp.arange(values.shape[0], dtype=jnp.int32) % 2 == 1
    return jnp.where(reverse_strand[:, None, None], values[:, ::-1], values)

def reference(inputs, first_depthwise_taps, second_depthwise_taps, first_pointwise_matrix, second_pointwise_matrix, head_weight, pred_cotangent, trunk_cotangent):
    first_block_output, first_block_backward = residual_block_forward(inputs, first_depthwise_taps, first_pointwise_matrix, DILATION_FIRST)
    second_block_output, second_block_backward = residual_block_forward(first_block_output, second_depthwise_taps, second_pointwise_matrix, DILATION_SECOND)
    top_values = orient(second_block_output[:, START:START + CROP].astype(jnp.float32))
    features, gelu_back = jax.vjp(jax.nn.gelu, top_values)
    features = features.astype(jnp.bfloat16)
    logits = product(features, head_weight)
    prediction = jax.nn.softplus(logits).astype(jnp.bfloat16)
    grad_logit = (pred_cotangent.astype(jnp.float32) * jax.nn.sigmoid(logits)).astype(jnp.bfloat16)
    flat_features = features.reshape(-1, D)
    flat_grads = grad_logit.reshape(-1, TRACKS)
    grad_head = jnp.dot(flat_features.T, flat_grads, preferred_element_type=jnp.float32)
    grad_features = product_back(grad_logit, head_weight)
    grad_kept = rounded_length(gelu_back(grad_features)[0]).astype(jnp.float32)
    placed = jnp.pad(orient(grad_kept), ((0, 0), (START, BINS - START - CROP), (0, 0)))
    second_block_gradient = rounded_length(placed + trunk_cotangent.astype(jnp.float32))
    first_block_gradient = rounded_length(residual_block_backward(second_block_gradient, second_depthwise_taps, second_pointwise_matrix, DILATION_SECOND, second_block_backward))
    input_gradient_rows = residual_block_backward(first_block_gradient, first_depthwise_taps, first_pointwise_matrix, DILATION_FIRST, first_block_backward)
    return (prediction, second_block_output, input_gradient_rows, grad_head)
```

```python
import jax
import jax.numpy as jnp
from jax import lax
from jax.sharding import PartitionSpec as P

DILATION_FIRST = 4
DILATION_SECOND = 8
HALO = 16
EPSILON = 1e-06

SHARES_BY_ROUND = ((0, 3, 6), (1, 4, 7), (2, 5, 8), (-1, 2, 5))
FIRST_ROWS = ((0, 16, 48), (80, 112, 128))
WINDOW_STARTS = (224, 368, 0, 240, 368, 32, 240, 384)


def norm_gelu(values):
    scaled = values * lax.rsqrt(jnp.mean(values * values, axis=-1, keepdims=True) + EPSILON)
    return jax.nn.gelu(scaled)


def convolve(values, taps, dilation):
    length = values.shape[0] - 2 * dilation
    values = values.astype(jnp.float32)
    return (
        taps[0] * values[:length]
        + taps[1] * values[dilation : dilation + length]
        + taps[2] * values[2 * dilation :]
    )


def product(rows, matrix):
    return jnp.dot(rows, matrix, preferred_element_type=jnp.float32)


def product_back(rows, matrix):
    return lax.dot_general(
        rows, matrix, (((1,), (1,)), ((), ())), preferred_element_type=jnp.float32
    )


def block_forward(rows, taps, matrix, dilation, keep=None):
    values = rows.astype(jnp.float32)
    activation = norm_gelu(values).astype(jnp.bfloat16)
    if keep is not None:
        activation = jnp.where(keep, activation, jnp.zeros((), activation.dtype))
    convolved = convolve(activation, taps, dilation).astype(jnp.bfloat16)
    inner = values[dilation : values.shape[0] - dilation]
    return (inner + product(convolved, matrix)).astype(jnp.bfloat16)


def block_backward(gradient, rows, taps, matrix, dilation):
    back = product_back(gradient, matrix).astype(jnp.bfloat16)
    activation_gradient = convolve(back, taps[::-1], dilation)
    inner = gradient[dilation : gradient.shape[0] - dilation].astype(jnp.float32)
    _, pull = jax.vjp(norm_gelu, rows.astype(jnp.float32))
    return inner + pull(activation_gradient)[0]


def routes(seq, trk, first_block):
    tables = []
    for by_block in SHARES_BY_ROUND:
        table = []
        for block in range(-1, seq * 3 // 8 + 1):
            share = 8 * (block // 3) + by_block[block % 3]
            if not 0 <= share < seq:
                continue
            for z in range(trk):
                target = share if z % 2 == 0 else seq - 1 - share
                table.append(((first_block + block) * trk + z, target * trk + z))
        tables.append(table)
    return tables


def on_device(
    inputs,
    first_taps,
    second_taps,
    first_matrix,
    second_matrix,
    head_weight,
    pred_cotangent,
    trunk_cotangent,
):
    seq, trk = lax.axis_size("seq"), lax.axis_size("trk")
    position, z = lax.axis_index("seq"), lax.axis_index("trk")
    reverse = z % 2 == 1
    both = ("seq", "trk")
    rows, cotangent = inputs[0], trunk_cotangent[0]
    local = rows.shape[0]
    share = local * 3 // 8
    first_block = 5 * seq // 16
    tables = routes(seq, trk, first_block)
    phase = (position + 3 * seq - first_block) % 3
    place = jnp.where(reverse, seq - 1 - position, position) % 8

    rounds = []
    for table, firsts in zip(tables[:2], FIRST_ROWS):
        first = jnp.asarray(firsts, jnp.int32)[phase]
        sent = lax.dynamic_slice_in_dim(rows, first, share + 2 * HALO, 0)
        rounds.append(lax.ppermute(sent, both, table))
    rounds.append(lax.ppermute(rows[local - 80 :], both, tables[2]))
    rounds.append(lax.ppermute(rows[:80], both, tables[3]))
    one, two, three, four = rounds
    up = [(i, i + 1) for i in range(seq - 1)]
    down = [(j, i) for i, j in up]
    ends = jnp.stack([rows[local - HALO :], cotangent[local - HALO :]])
    starts = jnp.stack([rows[:HALO], cotangent[:HALO]])
    before = lax.ppermute(ends, "seq", up)
    after = lax.ppermute(starts, "seq", down)

    pool = jnp.concatenate([three, four, three, one, two, four], axis=0)
    window = lax.dynamic_slice_in_dim(
        pool, jnp.asarray(WINDOW_STARTS, jnp.int32)[place], share + 2 * HALO, 0
    )
    middle = block_forward(window, first_taps, first_matrix, DILATION_FIRST)
    spare = HALO - DILATION_FIRST - DILATION_SECOND
    middle = middle[spare : middle.shape[0] - spare]
    kept = block_forward(middle, second_taps, second_matrix, DILATION_SECOND).astype(jnp.float32)
    features, gelu_back = jax.vjp(jax.nn.gelu, kept)
    features = features.astype(jnp.bfloat16)
    features = jnp.where(reverse, features[::-1], features)

    def shifted(array, step):
        return lax.ppermute(array, "trk", [(i, (i + step) % trk) for i in range(trk)])

    others = [features, shifted(features, 3), shifted(features, 2), shifted(features, 1)]
    gathered = lax.dynamic_slice_in_dim(
        jnp.concatenate(others + others[:3], axis=0), (trk - z) % trk * share, trk * share, 0
    )

    extended = jnp.concatenate([before[0], rows, after[0]], axis=0)
    own_middle = block_forward(extended, first_taps, first_matrix, DILATION_FIRST)
    own_middle = own_middle[spare : own_middle.shape[0] - spare]
    bins = position * local - DILATION_SECOND + jnp.arange(own_middle.shape[0], dtype=jnp.int32)
    inside = ((bins >= 0) & (bins < seq * local))[:, None]
    trunk_output = block_forward(
        own_middle, second_taps, second_matrix, DILATION_SECOND, inside
    )

    logits = product(gathered, head_weight)
    prediction = jax.nn.softplus(logits).astype(jnp.bfloat16)
    flat_cotangent = pred_cotangent.reshape(-1, pred_cotangent.shape[-1])
    grad_logit = (flat_cotangent.astype(jnp.float32) * jax.nn.sigmoid(logits)).astype(jnp.bfloat16)
    grad_head = lax.psum_scatter(
        lax.dot_general(
            gathered, grad_logit, (((0,), (0,)), ((), ())), preferred_element_type=jnp.float32
        ).astype(jnp.bfloat16),
        "seq",
        scatter_dimension=0,
        tiled=True,
    ).astype(jnp.float32)
    partials = product_back(grad_logit, head_weight).astype(jnp.bfloat16)

    def partial_of(step):
        return lax.dynamic_slice_in_dim(partials, (z + step) % trk * share, share, 0)

    grad_features = partial_of(0).astype(jnp.float32)
    for step in range(1, trk):
        grad_features = grad_features + shifted(partial_of(step), step).astype(jnp.float32)
    grad_features = jnp.where(reverse, grad_features[::-1], grad_features)
    grad_kept = gelu_back(grad_features)[0].astype(jnp.bfloat16)

    tables = [[(j, i) for i, j in table] for table in tables]
    one = lax.ppermute(grad_kept, both, tables[0])
    two = lax.ppermute(grad_kept, both, tables[1])
    three = lax.ppermute(grad_kept[:80], both, tables[2])
    four = lax.ppermute(grad_kept[share - 80 :], both, tables[3])
    pool = jnp.concatenate([four, one, two, three], axis=0)
    placed = lax.dynamic_slice_in_dim(pool, 64 - 32 * phase, local + 2 * HALO, 0)
    own_cotangent = jnp.concatenate([before[1], cotangent, after[1]], axis=0)
    second_gradient = (placed.astype(jnp.float32) + own_cotangent.astype(jnp.float32)).astype(
        jnp.bfloat16
    )
    first_gradient = block_backward(
        second_gradient, own_middle, second_taps, second_matrix, DILATION_SECOND
    ).astype(jnp.bfloat16)
    first_gradient = jnp.where(inside, first_gradient, jnp.zeros((), first_gradient.dtype))
    margin = DILATION_SECOND - DILATION_FIRST
    first_gradient = first_gradient[margin : first_gradient.shape[0] - margin]
    input_gradient = block_backward(
        first_gradient, rows, first_taps, first_matrix, DILATION_FIRST
    )
    return (
        prediction.reshape(pred_cotangent.shape),
        trunk_output[None],
        input_gradient[None],
        grad_head,
    )


def solution(mesh):
    in_specs = (
        P("trk", "seq", None),
        P(),
        P(),
        P(),
        P(),
        P(None, "trk"),
        P(None, "seq", "trk"),
        P("trk", "seq", None),
    )
    out_specs = (
        P(None, "seq", "trk"),
        P("trk", "seq", None),
        P("trk", "seq", None),
        P("seq", "trk"),
    )
    return jax.shard_map(
        on_device, mesh=mesh, in_specs=in_specs, out_specs=out_specs, check_vma=False
    )
```

```python
import jax
import jax.numpy as jnp
from jax import lax
from jax.experimental import pallas as pl
from jax.experimental.pallas import tpu as pltpu
from jax.sharding import PartitionSpec as P

DILATION_FIRST = 4
DILATION_SECOND = 8
HALO = 16
EPSILON = 1e-06

SHARES_BY_ROUND = ((0, 3, 6), (1, 4, 7), (2, 5, 8), (-1, 2, 5))
FIRST_ROWS = ((0, 16, 48), (80, 112, 128))
WINDOW_STARTS = (224, 368, 0, 240, 368, 32, 240, 384)


def norm_gelu(values):
    scaled = values * lax.rsqrt(jnp.mean(values * values, axis=-1, keepdims=True) + EPSILON)
    return jax.nn.gelu(scaled)


def convolve(values, taps, dilation):
    length = values.shape[0] - 2 * dilation
    values = values.astype(jnp.float32)
    return (
        taps[0] * values[:length]
        + taps[1] * values[dilation : dilation + length]
        + taps[2] * values[2 * dilation :]
    )


def product(rows, matrix):
    return jnp.dot(rows, matrix, preferred_element_type=jnp.float32)


def product_back(rows, matrix):
    return lax.dot_general(
        rows, matrix, (((1,), (1,)), ((), ())), preferred_element_type=jnp.float32
    )


def block_forward(rows, taps, matrix, dilation, keep=None):
    values = rows.astype(jnp.float32)
    activation = norm_gelu(values).astype(jnp.bfloat16)
    if keep is not None:
        activation = jnp.where(keep, activation, jnp.zeros((), activation.dtype))
    convolved = convolve(activation, taps, dilation).astype(jnp.bfloat16)
    inner = values[dilation : values.shape[0] - dilation]
    return (inner + product(convolved, matrix)).astype(jnp.bfloat16)


def block_backward(gradient, rows, taps, matrix, dilation):
    back = product_back(gradient, matrix).astype(jnp.bfloat16)
    activation_gradient = convolve(back, taps[::-1], dilation)
    inner = gradient[dilation : gradient.shape[0] - dilation].astype(jnp.float32)
    _, pull = jax.vjp(norm_gelu, rows.astype(jnp.float32))
    return inner + pull(activation_gradient)[0]


def routes(seq, trk, first_block):
    tables = []
    for by_block in SHARES_BY_ROUND:
        table = []
        for block in range(-1, seq * 3 // 8 + 1):
            share = 8 * (block // 3) + by_block[block % 3]
            if not 0 <= share < seq:
                continue
            for z in range(trk):
                target = share if z % 2 == 0 else seq - 1 - share
                table.append(((first_block + block) * trk + z, target * trk + z))
        tables.append(table)
    return tables


def outer_kernel(at_ref, mine_ref, theirs_ref, grad_ref, their_grad_ref, across_ref, along_ref):
    step = pl.program_id(0)
    dims = (((0,), (0,)), ((), ()))
    total = lax.dot_general(mine_ref[...], grad_ref[...], dims, preferred_element_type=jnp.float32)
    total += lax.dot_general(
        theirs_ref[...], their_grad_ref[...], dims, preferred_element_type=jnp.float32
    )
    total = total.astype(jnp.bfloat16)
    size = pl.num_programs(0)
    rows = across_ref.shape[2]
    relative_x = (step + size - at_ref[0]) % size
    for y in range(4):
        relative_y = (y + 4 - at_ref[1]) % 4
        across_ref[relative_x, relative_y] = total[2 * rows * y : 2 * rows * y + rows]
        along_ref[relative_y, relative_x] = total[2 * rows * y + rows : 2 * rows * (y + 1)]


def outer_products(at, mine, theirs, grad, their_grad):
    bins, channels = mine.shape
    tracks = grad.shape[1]
    features = pl.BlockSpec((bins, channels // 4), lambda i, at: (0, i))
    whole = pl.BlockSpec((bins, tracks), lambda i, at: (0, 0))
    shape = (4, 4, channels // 32, tracks)
    result = pl.BlockSpec(shape, lambda i, at: (0, 0, 0, 0))
    return pl.pallas_call(
        outer_kernel,
        out_shape=[jax.ShapeDtypeStruct(shape, jnp.bfloat16)] * 2,
        grid_spec=pltpu.PrefetchScalarGridSpec(
            num_scalar_prefetch=1,
            grid=(4,),
            in_specs=[features, features, whole, whole],
            out_specs=[result, result],
        ),
        compiler_params=pltpu.CompilerParams(dimension_semantics=("arbitrary",)),
        name="outer_products",
    )(at, mine, theirs, grad, their_grad)


def moves(seq):
    def table(dx, dy):
        pairs = []
        for i in range(seq):
            x, y, core = i // 8, i // 2 % 4, i % 2
            pairs.append((i, (x + dx) % 4 * 8 + (y + dy) % 4 * 2 + core))
        return pairs

    return lambda step: table(step, 0), lambda step: table(0, step)


def widen(array):
    return array.astype(jnp.float32)


def ring_sum(pieces, move):
    half = pieces.shape[1] // 2
    forth = lax.ppermute(pieces[2][:half], "seq", move(1))
    back = lax.ppermute(pieces[2][half:], "seq", move(3))
    nexts = jnp.concatenate(
        [(widen(pieces[1][:half]) + widen(forth)).astype(jnp.bfloat16), pieces[1][half:]]
    )
    lasts = jnp.concatenate(
        [pieces[3][:half], (widen(pieces[3][half:]) + widen(back)).astype(jnp.bfloat16)]
    )
    forth = lax.ppermute(nexts, "seq", move(1))
    back = lax.ppermute(lasts, "seq", move(3))
    return widen(pieces[0]) + widen(forth) + widen(back)


def direct_sum(total, move):
    pieces = total.astype(jnp.bfloat16)
    result = total[0]
    for step in (1, 2, 3):
        result = result + widen(lax.ppermute(pieces[step], "seq", move(step)))
    return result


def on_device(
    inputs,
    first_taps,
    second_taps,
    first_matrix,
    second_matrix,
    head_weight,
    pred_cotangent,
    trunk_cotangent,
):
    seq, trk = lax.axis_size("seq"), lax.axis_size("trk")
    position, z = lax.axis_index("seq"), lax.axis_index("trk")
    reverse = z % 2 == 1
    both = ("seq", "trk")
    rows, cotangent = inputs[0], trunk_cotangent[0]
    local = rows.shape[0]
    share = local * 3 // 8
    first_block = 5 * seq // 16
    tables = routes(seq, trk, first_block)
    phase = (position + 3 * seq - first_block) % 3
    place = jnp.where(reverse, seq - 1 - position, position) % 8

    rounds = []
    for table, firsts in zip(tables[:2], FIRST_ROWS):
        first = jnp.asarray(firsts, jnp.int32)[phase]
        sent = lax.dynamic_slice_in_dim(rows, first, share + 2 * HALO, 0)
        rounds.append(lax.ppermute(sent, both, table))
    rounds.append(lax.ppermute(rows[local - 80 :], both, tables[2]))
    rounds.append(lax.ppermute(rows[:80], both, tables[3]))
    one, two, three, four = rounds
    up = [(i, i + 1) for i in range(seq - 1)]
    down = [(j, i) for i, j in up]
    ends = jnp.stack([rows[local - HALO :], cotangent[local - HALO :]])
    starts = jnp.stack([rows[:HALO], cotangent[:HALO]])
    before = lax.ppermute(ends, "seq", up)
    after = lax.ppermute(starts, "seq", down)

    pool = jnp.concatenate([three, four, three, one, two, four], axis=0)
    window = lax.dynamic_slice_in_dim(
        pool, jnp.asarray(WINDOW_STARTS, jnp.int32)[place], share + 2 * HALO, 0
    )
    middle = block_forward(window, first_taps, first_matrix, DILATION_FIRST)
    spare = HALO - DILATION_FIRST - DILATION_SECOND
    middle = middle[spare : middle.shape[0] - spare]
    kept = block_forward(middle, second_taps, second_matrix, DILATION_SECOND).astype(jnp.float32)
    features, gelu_back = jax.vjp(jax.nn.gelu, kept)
    features = features.astype(jnp.bfloat16)
    features = jnp.where(reverse, features[::-1], features)

    def shifted(array, step):
        return lax.ppermute(array, "trk", [(i, (i + step) % trk) for i in range(trk)])

    others = [features, shifted(features, 3), shifted(features, 2), shifted(features, 1)]
    gathered = lax.dynamic_slice_in_dim(
        jnp.concatenate(others + others[:3], axis=0), (trk - z) % trk * share, trk * share, 0
    )

    extended = jnp.concatenate([before[0], rows, after[0]], axis=0)
    own_middle = block_forward(extended, first_taps, first_matrix, DILATION_FIRST)
    own_middle = own_middle[spare : own_middle.shape[0] - spare]
    bins = position * local - DILATION_SECOND + jnp.arange(own_middle.shape[0], dtype=jnp.int32)
    inside = ((bins >= 0) & (bins < seq * local))[:, None]
    trunk_output = block_forward(
        own_middle, second_taps, second_matrix, DILATION_SECOND, inside
    )

    logits = product(gathered, head_weight)
    prediction = jax.nn.softplus(logits).astype(jnp.bfloat16)
    flat_cotangent = pred_cotangent.reshape(-1, pred_cotangent.shape[-1])
    grad_logit = (flat_cotangent.astype(jnp.float32) * jax.nn.sigmoid(logits)).astype(jnp.bfloat16)
    core = position % 2
    partner = [(i, i ^ 1) for i in range(seq)]
    tracks = grad_logit.shape[1] // 2
    halves = grad_logit[:, :tracks], grad_logit[:, tracks:]
    own_half = jnp.where(core == 0, halves[0], halves[1])
    their_half = lax.ppermute(jnp.where(core == 0, halves[1], halves[0]), "seq", partner)
    at = jnp.stack([position // 8, position // 2 % 4]).astype(jnp.int32)
    across, along = outer_products(
        at, gathered, lax.ppermute(gathered, "seq", partner), own_half, their_half
    )
    by_x, by_y = moves(seq)
    even = direct_sum(ring_sum(across, by_x), by_y)
    odd = direct_sum(ring_sum(along, by_y), by_x)
    sent = jnp.where(core == 0, odd, even).astype(jnp.bfloat16)
    swapped = widen(lax.ppermute(sent, "seq", partner))
    grad_head = jnp.where(
        core == 0,
        jnp.concatenate([even, swapped], axis=1),
        jnp.concatenate([swapped, odd], axis=1),
    )
    partials = product_back(grad_logit, head_weight).astype(jnp.bfloat16)

    def partial_of(step):
        return lax.dynamic_slice_in_dim(partials, (z + step) % trk * share, share, 0)

    grad_features = partial_of(0).astype(jnp.float32)
    for step in range(1, trk):
        grad_features = grad_features + shifted(partial_of(step), step).astype(jnp.float32)
    grad_features = jnp.where(reverse, grad_features[::-1], grad_features)
    grad_kept = gelu_back(grad_features)[0].astype(jnp.bfloat16)

    tables = [[(j, i) for i, j in table] for table in tables]
    one = lax.ppermute(grad_kept, both, tables[0])
    two = lax.ppermute(grad_kept, both, tables[1])
    three = lax.ppermute(grad_kept[:80], both, tables[2])
    four = lax.ppermute(grad_kept[share - 80 :], both, tables[3])
    pool = jnp.concatenate([four, one, two, three], axis=0)
    placed = lax.dynamic_slice_in_dim(pool, 64 - 32 * phase, local + 2 * HALO, 0)
    own_cotangent = jnp.concatenate([before[1], cotangent, after[1]], axis=0)
    second_gradient = (placed.astype(jnp.float32) + own_cotangent.astype(jnp.float32)).astype(
        jnp.bfloat16
    )
    first_gradient = block_backward(
        second_gradient, own_middle, second_taps, second_matrix, DILATION_SECOND
    ).astype(jnp.bfloat16)
    first_gradient = jnp.where(inside, first_gradient, jnp.zeros((), first_gradient.dtype))
    margin = DILATION_SECOND - DILATION_FIRST
    first_gradient = first_gradient[margin : first_gradient.shape[0] - margin]
    input_gradient = block_backward(
        first_gradient, rows, first_taps, first_matrix, DILATION_FIRST
    )
    return (
        prediction.reshape(pred_cotangent.shape),
        trunk_output[None],
        input_gradient[None],
        grad_head,
    )


def solution(mesh):
    in_specs = (
        P("trk", "seq", None),
        P(),
        P(),
        P(),
        P(),
        P(None, "trk"),
        P(None, "seq", "trk"),
        P("trk", "seq", None),
    )
    out_specs = (
        P(None, "seq", "trk"),
        P("trk", "seq", None),
        P("trk", "seq", None),
        P("seq", "trk"),
    )
    return jax.shard_map(
        on_device, mesh=mesh, in_specs=in_specs, out_specs=out_specs, check_vma=False
    )
```

```python
import jax
import jax.numpy as jnp
from jax import lax
from jax.experimental import pallas as pl
from jax.experimental.pallas import tpu as pltpu
from jax.sharding import PartitionSpec as P

DILATION_FIRST = 4
DILATION_SECOND = 8
HALO = 16
EPSILON = 1e-06
STEP = 16
COLUMNS = 512

SHARES_BY_ROUND = ((0, 3, 6), (1, 4, 7), (2, 5, 8), (-1, 2, 5))
FIRST_ROWS = ((0, 16, 48), (80, 112, 128))
PIECES = (
    ((2, 64, 80), (0, 0, 112)),
    ((1, 0, 128),),
    ((2, 0, 80), (3, 0, 48)),
    ((0, 0, 128),),
    ((1, 0, 128),),
    ((2, 32, 80), (3, 0, 80)),
    ((0, 0, 128),),
    ((1, 16, 128), (3, 0, 16)),
)


BF16, F32 = jnp.bfloat16, jnp.float32
VMEM = pl.BlockSpec(memory_space=pltpu.VMEM)
SMEM = pl.BlockSpec(memory_space=pltpu.SMEM)
ANY = pl.BlockSpec(memory_space=pl.ANY)


def shaped(rows, columns, dtype=BF16):
    return jax.ShapeDtypeStruct((rows, columns), dtype)


def gelu_slope(values):
    k, c = 0.7978845608028654, 0.044715
    square = values * values
    t = jnp.tanh(k * values * (1.0 + c * square))
    return 0.5 * (1.0 + t) + 0.5 * values * (1.0 - t * t) * (k * (1.0 + 3.0 * c * square))


def inverse_norm(values):
    return lax.rsqrt(jnp.mean(values * values, axis=-1, keepdims=True) + EPSILON)


def for_chunks(count, body):
    def step(k, carry):
        body(pl.multiple_of(k * STEP, STEP))
        return carry

    lax.fori_loop(0, count, step, 0)


def span(start, offset=0, size=STEP):
    return pl.ds(pl.multiple_of(start + offset, 8), size)


def weighted(values_ref, taps_ref, at, offsets):
    base = min(offsets) // 8 * 8
    block = values_ref[span(at, base, 2 * STEP), :]
    total = taps_ref[0:1, :] * block[offsets[0] - base : offsets[0] - base + STEP]
    total += taps_ref[1:2, :] * block[offsets[1] - base : offsets[1] - base + STEP]
    return total + taps_ref[2:3, :] * block[offsets[2] - base : offsets[2] - base + STEP]


def activate(values_ref, out_ref, rows, inside=None):
    def body(at):
        values = values_ref[span(at), :]
        result = jax.nn.gelu(values * inverse_norm(values)).astype(BF16).astype(F32)
        if inside is not None:
            result = jnp.where(inside(at, result.shape), result, 0.0)
        out_ref[span(at), :] = result

    for_chunks(rows // STEP, body)


def convolve(values_ref, taps_ref, offsets, out_ref, rows):
    def body(at):
        out_ref[span(at), :] = weighted(values_ref, taps_ref, at, offsets).astype(BF16)

    for_chunks(rows // STEP, body)


def product(rows, matrix):
    return jnp.dot(rows, matrix, preferred_element_type=F32)


def product_back(rows, matrix):
    return lax.dot_general(rows, matrix, (((1,), (1,)), ((), ())), preferred_element_type=F32)


def flipped(flag, rows, values):
    row = lax.broadcasted_iota(jnp.int32, (rows, rows), 0)
    column = lax.broadcasted_iota(jnp.int32, (rows, rows), 1)
    target = jnp.where(flag == 1, rows - 1 - row, row)
    return product((column == target).astype(BF16), values).astype(BF16)


def cut_kernel(first_ref, rows_ref, cotangent_ref, one, two, three, four, ends, starts):
    local = rows_ref.shape[0]
    size = one.shape[0]
    one[...] = rows_ref[pl.ds(pl.multiple_of(first_ref[0], 16), size), :]
    two[...] = rows_ref[pl.ds(pl.multiple_of(first_ref[1], 16), size), :]
    three[...] = rows_ref[local - three.shape[0] :, :]
    four[...] = rows_ref[: four.shape[0], :]
    ends[:HALO, :] = rows_ref[local - HALO :, :]
    ends[HALO:, :] = cotangent_ref[local - HALO :, :]
    starts[:HALO, :] = rows_ref[:HALO, :]
    starts[HALO:, :] = cotangent_ref[:HALO, :]


def cut(firsts, rows, cotangent, size):
    d = rows.shape[1]
    sizes = (size, size, 80, 80, 2 * HALO, 2 * HALO)
    return pl.pallas_call(
        cut_kernel,
        out_shape=[shaped(n, d) for n in sizes],
        in_specs=[SMEM, VMEM, VMEM],
        out_specs=[VMEM] * 6,
        name="cut",
    )(firsts, rows, cotangent)


def window_kernel(
    at_ref, one, two, three, four, taps_ref, taps2_ref, matrix_hbm, matrix2_hbm,
    kept_ref, features_ref,
    values, active, convolved, matrix, matrix2, sems,
):
    loads = [
        pltpu.make_async_copy(matrix_hbm, matrix, sems.at[0]),
        pltpu.make_async_copy(matrix2_hbm, matrix2, sems.at[1]),
    ]
    for load in loads:
        load.start()
    rounds = (one, two, three, four)
    for place, pieces in enumerate(PIECES):

        @pl.when(at_ref[0] == place)
        def _():
            row = 0
            for index, first, last in pieces:
                values[row : row + last - first, :] = rounds[index][first:last, :].astype(F32)
                row += last - first

    size = values.shape[0]
    d = values.shape[1]
    share = size - 2 * HALO
    active[:8, :] = jnp.zeros((8, d), F32)
    active[size + 8 :, :] = jnp.zeros((8, d), F32)
    inner = active.at[8 : size + 8, :]
    activate(values, inner, size)
    q = DILATION_FIRST
    convolve(active, taps_ref, (8 - q, 8, 8 + q), convolved, size)
    loads[0].wait()
    for n in range(0, d, COLUMNS):
        part = values[:, n : n + COLUMNS] + product(convolved[...], matrix[:, n : n + COLUMNS])
        values[:, n : n + COLUMNS] = part.astype(BF16).astype(F32)
    activate(values, inner, size)
    q = DILATION_SECOND
    convolve(active, taps2_ref, (8 + HALO - q, 8 + HALO, 8 + HALO + q), convolved, share)
    loads[1].wait()
    for n in range(0, d, COLUMNS):
        part = values[HALO : HALO + share, n : n + COLUMNS] + product(
            convolved[:share, :], matrix2[:, n : n + COLUMNS]
        )
        kept = part.astype(BF16)
        features = jax.nn.gelu(kept.astype(F32)).astype(BF16)
        kept_ref[:, n : n + COLUMNS] = flipped(at_ref[1], share, kept)
        features_ref[:, n : n + COLUMNS] = flipped(at_ref[1], share, features)


def window_forward(at, rounds, taps, taps2, matrix, matrix2):
    size, d = rounds[0].shape
    share = size - 2 * HALO
    return pl.pallas_call(
        window_kernel,
        out_shape=[shaped(share, d)] * 2,
        in_specs=[SMEM] + [VMEM] * 6 + [ANY] * 2,
        out_specs=[VMEM] * 2,
        scratch_shapes=[
            pltpu.VMEM((size, d), F32),
            pltpu.VMEM((size + 16, d), F32),
            pltpu.VMEM((size, d), BF16),
            pltpu.VMEM((d, d), BF16),
            pltpu.VMEM((d, d), BF16),
            pltpu.SemaphoreType.DMA((2,)),
        ],
        name="window_forward",
    )(at, *rounds, taps, taps2, matrix, matrix2)


def inside_of(at_ref, local):
    def inside(at, shape):
        row = at + lax.broadcasted_iota(jnp.int32, shape, 0)
        return (row >= at_ref[0]) & (row < at_ref[1])

    return inside


def own_kernel(
    at_ref, before, rows_ref, after, taps_ref, taps2_ref, matrix_hbm, matrix2_hbm,
    middle_ref, result_ref,
    values, active, convolved, matrix, matrix2, sems,
):
    loads = [
        pltpu.make_async_copy(matrix_hbm, matrix, sems.at[0]),
        pltpu.make_async_copy(matrix2_hbm, matrix2, sems.at[1]),
    ]
    for load in loads:
        load.start()
    local, d = rows_ref.shape
    wide = local + 2 * HALO
    middle = local + 2 * DILATION_SECOND
    edge = HALO - DILATION_SECOND
    values[:HALO, :] = before[:HALO, :].astype(F32)
    values[HALO : HALO + local, :] = rows_ref[...].astype(F32)
    values[HALO + local :, :] = after[:HALO, :].astype(F32)
    activate(values, active, wide)
    q = DILATION_FIRST
    convolve(active, taps_ref, (edge - q, edge, edge + q), convolved, middle)
    loads[0].wait()
    for n in range(0, d, COLUMNS):
        part = values[edge : edge + middle, n : n + COLUMNS] + product(
            convolved[...], matrix[:, n : n + COLUMNS]
        )
        part = part.astype(BF16)
        middle_ref[:, n : n + COLUMNS] = part
        values[:middle, n : n + COLUMNS] = part.astype(F32)
    activate(values, active, middle, inside_of(at_ref, local))
    q = DILATION_SECOND
    convolve(active, taps2_ref, (0, q, 2 * q), convolved, local)
    loads[1].wait()
    for n in range(0, d, COLUMNS):
        part = values[q : q + local, n : n + COLUMNS] + product(
            convolved[:local, :], matrix2[:, n : n + COLUMNS]
        )
        result_ref[:, n : n + COLUMNS] = part.astype(BF16)


def own_forward(at, before, rows, after, taps, taps2, matrix, matrix2):
    local, d = rows.shape
    wide, middle = local + 2 * HALO, local + 2 * DILATION_SECOND
    return pl.pallas_call(
        own_kernel,
        out_shape=[shaped(middle, d), shaped(local, d)],
        in_specs=[SMEM] + [VMEM] * 5 + [ANY] * 2,
        out_specs=[VMEM] * 2,
        scratch_shapes=[
            pltpu.VMEM((wide, d), F32),
            pltpu.VMEM((wide, d), F32),
            pltpu.VMEM((middle, d), BF16),
            pltpu.VMEM((d, d), BF16),
            pltpu.VMEM((d, d), BF16),
            pltpu.SemaphoreType.DMA((2,)),
        ],
        name="own_forward",
    )(at, before, rows, after, taps, taps2, matrix, matrix2)


def head_kernel(
    at_ref, features_ref, weight_ref, cotangent_ref,
    prediction_ref, sent_ref, kept_ref, own_ref, one_ref, two_ref, three_ref,
    total,
):
    step = pl.program_id(0)
    batch, share = cotangent_ref.shape[:2]
    for k in range(batch):
        sequence = (at_ref[1] + k) % batch
        rows = slice(k * share, (k + 1) * share)
        logits = product(features_ref[rows, :], weight_ref[...])
        small = jnp.exp(-jnp.abs(logits))
        softplus = jnp.maximum(logits, 0.0) + jnp.log1p(small)
        sigmoid = jnp.where(logits >= 0.0, 1.0, small) / (1.0 + small)
        prediction_ref[sequence] = softplus.astype(BF16)
        gradient = (cotangent_ref[sequence].astype(F32) * sigmoid).astype(BF16)

        @pl.when(step == 0)
        def _():
            sent_ref[rows, :] = gradient
            total[rows, :] = product_back(gradient, weight_ref[...])

        @pl.when(step == 1)
        def _():
            kept_ref[rows, :] = gradient
            result = total[rows, :] + product_back(gradient, weight_ref[...])
            out = (own_ref, one_ref, two_ref, three_ref)[k]
            out[...] = result.astype(out.dtype)


def head(at, features, weight, cotangent):
    batch, share, tracks = cotangent.shape
    half = tracks // 2
    bins, d = features.shape

    def turn(i, at):
        return (i + at[0] + 1) % 2

    block = pl.BlockSpec((batch, share, half), lambda i, at: (0, 0, turn(i, at)))
    flat = pl.BlockSpec((bins, half), lambda i, at: (0, 0))
    piece = pl.BlockSpec((share, d), lambda i, at: (0, 0))
    return pl.pallas_call(
        head_kernel,
        out_shape=[jax.ShapeDtypeStruct(cotangent.shape, BF16)]
        + [shaped(bins, half)] * 2
        + [shaped(share, d, F32)]
        + [shaped(share, d)] * 3,
        grid_spec=pltpu.PrefetchScalarGridSpec(
            num_scalar_prefetch=1,
            grid=(2,),
            in_specs=[
                pl.BlockSpec((bins, d), lambda i, at: (0, 0)),
                pl.BlockSpec((d, half), lambda i, at: (0, turn(i, at))),
                block,
            ],
            out_specs=[block, flat, flat] + [piece] * 4,
            scratch_shapes=[pltpu.VMEM((bins, d), F32)],
        ),
        compiler_params=pltpu.CompilerParams(dimension_semantics=("arbitrary",)),
        name="head",
    )(at, features, weight, cotangent)


def outer_kernel(at_ref, mine_ref, theirs_ref, grad_ref, their_grad_ref, out_ref):
    step = pl.program_id(0)
    dims = (((0,), (0,)), ((), ()))
    total = lax.dot_general(mine_ref[...], grad_ref[...], dims, preferred_element_type=F32)
    total += lax.dot_general(theirs_ref[...], their_grad_ref[...], dims, preferred_element_type=F32)
    total = total.astype(BF16)
    rows = out_ref.shape[2]
    relative_x = (step + 4 - at_ref[0]) % 4
    for y in range(4):
        relative_y = (y + 4 - at_ref[1]) % 4
        first = jnp.where(at_ref[2] == 0, relative_x, relative_y)
        second = jnp.where(at_ref[2] == 0, relative_y, relative_x)
        out_ref[first, second] = total[rows * y : rows * (y + 1)]


def outer_products(at, mine, theirs, grad, their_grad):
    bins, d = mine.shape
    tracks = grad.shape[1]
    features = pl.BlockSpec((bins, d // 4), lambda i, at: (0, i))
    whole = pl.BlockSpec((bins, tracks), lambda i, at: (0, 0))
    shape = (4, 4, d // 16, tracks)
    return pl.pallas_call(
        outer_kernel,
        out_shape=jax.ShapeDtypeStruct(shape, BF16),
        grid_spec=pltpu.PrefetchScalarGridSpec(
            num_scalar_prefetch=1,
            grid=(4,),
            in_specs=[features, features, whole, whole],
            out_specs=pl.BlockSpec(shape, lambda i, at: (0, 0, 0, 0)),
        ),
        compiler_params=pltpu.CompilerParams(dimension_semantics=("arbitrary",)),
        name="outer_products",
    )(at, mine, theirs, grad, their_grad)


def kept_kernel(at_ref, own, one, two, three, kept_ref, result_ref, initial_ref, last_ref):
    total = own[...] + one[...].astype(F32) + two[...].astype(F32) + three[...].astype(F32)
    share = total.shape[0]
    gradient = (gelu_slope(kept_ref[...].astype(F32)) * total).astype(BF16)
    gradient = flipped(at_ref[1], share, gradient)
    result_ref[...] = gradient
    initial_ref[...] = gradient[: initial_ref.shape[0]]
    last_ref[...] = gradient[share - last_ref.shape[0] :]


def kept_gradient(at, pieces, kept):
    share, d = kept.shape
    return pl.pallas_call(
        kept_kernel,
        out_shape=[shaped(share, d), shaped(80, d), shaped(80, d)],
        in_specs=[SMEM] + [VMEM] * 5,
        out_specs=[VMEM] * 3,
        name="kept_gradient",
    )(at, *pieces, kept)


def pull_back(values_ref, offset, back_ref, taps_ref, offsets, gradient_ref, shift, write, rows):
    def body(at):
        values = values_ref[span(at, offset), :].astype(F32)
        inner = weighted(back_ref, taps_ref, at, offsets)
        inverse = inverse_norm(values)
        scaled = values * inverse
        inner = gelu_slope(scaled) * inner
        along = jnp.mean(scaled * inner, axis=-1, keepdims=True)
        write(at, gradient_ref[span(at, shift), :] + inverse * (inner - scaled * along))

    for_chunks(rows // STEP, body)


def backward_kernel(
    at_ref, one, two, three, four, before, cotangent_ref, after, middle_ref, rows_ref,
    taps_ref, taps2_ref, matrix_hbm, matrix2_hbm,
    result_ref,
    pool, gradient, wide_gradient, back, matrix, matrix2, sems,
):
    loads = [
        pltpu.make_async_copy(matrix2_hbm, matrix2, sems.at[0]),
        pltpu.make_async_copy(matrix_hbm, matrix, sems.at[1]),
    ]
    for load in loads:
        load.start()
    local, d = rows_ref.shape
    wide = local + 2 * HALO
    middle = local + 2 * DILATION_SECOND
    edge = HALO - DILATION_SECOND
    row = 0
    for piece in (four, one, two, three):
        pool[row : row + piece.shape[0], :] = piece[...]
        row += piece.shape[0]
    wide_gradient[:HALO, :] = before[HALO:, :].astype(F32)
    wide_gradient[HALO : HALO + local, :] = cotangent_ref[...].astype(F32)
    wide_gradient[HALO + local :, :] = after[HALO:, :].astype(F32)

    def place(at):
        placed = pool[pl.ds(pl.multiple_of(at_ref[2] + at, 16), STEP), :].astype(F32)
        total = (placed + wide_gradient[span(at), :]).astype(BF16)
        gradient[span(at), :] = total
        wide_gradient[span(at), :] = total.astype(F32)

    for_chunks(wide // STEP, place)
    loads[0].wait()
    for n in range(0, d, COLUMNS):
        part = product_back(gradient[...], matrix2[n : n + COLUMNS, :])
        back[:, n : n + COLUMNS] = part.astype(BF16).astype(F32)
    inside = inside_of(at_ref, local)

    def write_middle(at, total):
        total = jnp.where(inside(at, total.shape), total, 0.0).astype(BF16)
        gradient[span(at), :] = total
        wide_gradient[span(at), :] = total.astype(F32)

    q = DILATION_SECOND
    pull_back(
        middle_ref, 0, back, taps2_ref, (edge + q, edge, edge - q), wide_gradient, edge,
        write_middle, middle,
    )
    loads[1].wait()
    for n in range(0, d, COLUMNS):
        part = product_back(gradient[:middle, :], matrix[n : n + COLUMNS, :])
        back[:middle, n : n + COLUMNS] = part.astype(BF16).astype(F32)

    def write_last(at, total):
        result_ref[span(at), :] = total

    edge, q = DILATION_SECOND, DILATION_FIRST
    pull_back(
        rows_ref, 0, back, taps_ref, (edge + q, edge, edge - q), wide_gradient, edge,
        write_last, local,
    )


def backward(at, rounds, before, cotangent, after, middle, rows, taps, taps2, matrix, matrix2):
    local, d = rows.shape
    wide = local + 2 * HALO
    return pl.pallas_call(
        backward_kernel,
        out_shape=shaped(local, d, F32),
        in_specs=[SMEM] + [VMEM] * 11 + [ANY] * 2,
        out_specs=VMEM,
        scratch_shapes=[
            pltpu.VMEM((2 * 80 + local * 3 // 4, d), BF16),
            pltpu.VMEM((wide, d), BF16),
            pltpu.VMEM((wide, d), F32),
            pltpu.VMEM((wide, d), F32),
            pltpu.VMEM((d, d), BF16),
            pltpu.VMEM((d, d), BF16),
            pltpu.SemaphoreType.DMA((2,)),
        ],
        name="backward",
    )(at, *rounds, before, cotangent, after, middle, rows, taps, taps2, matrix, matrix2)


def routes(seq, trk, first_block):
    tables = []
    for by_block in SHARES_BY_ROUND:
        table = []
        for block in range(-1, seq * 3 // 8 + 1):
            share = 8 * (block // 3) + by_block[block % 3]
            if not 0 <= share < seq:
                continue
            for z in range(trk):
                target = share if z % 2 == 0 else seq - 1 - share
                table.append(((first_block + block) * trk + z, target * trk + z))
        tables.append(table)
    return tables


def chip_moves(seq, across, step):
    pairs = []
    for i in range(seq):
        x, y, core = i // 8, i // 2 % 4, i % 2
        if (core == 0) == across:
            x = (x + step) % 4
        else:
            y = (y + step) % 4
        pairs.append((i, x * 8 + y * 2 + core))
    return pairs


def widen(array):
    return array.astype(F32)


def on_device(
    inputs,
    first_taps,
    second_taps,
    first_matrix,
    second_matrix,
    head_weight,
    pred_cotangent,
    trunk_cotangent,
):
    seq, trk = lax.axis_size("seq"), lax.axis_size("trk")
    position, z = lax.axis_index("seq"), lax.axis_index("trk")
    reverse = z % 2
    both = ("seq", "trk")
    rows, cotangent = inputs[0], trunk_cotangent[0]
    local = rows.shape[0]
    share = local * 3 // 8
    first_block = 5 * seq // 16
    tables = routes(seq, trk, first_block)
    phase = (position + 3 * seq - first_block) % 3
    place = jnp.where(reverse == 1, seq - 1 - position, position) % 8
    core = position % 2
    spots = jnp.stack([position // 8, position // 2 % 4, core]).astype(jnp.int32)
    edge = DILATION_SECOND
    limits = jnp.stack(
        [
            jnp.where(position == 0, edge, 0),
            jnp.where(position == seq - 1, edge + local, local + 2 * edge),
            64 - 32 * phase,
        ]
    ).astype(jnp.int32)
    sides = jnp.stack([place, reverse]).astype(jnp.int32)
    turns = jnp.stack([core, z]).astype(jnp.int32)

    firsts = jnp.asarray(FIRST_ROWS, jnp.int32)[:, phase]
    *sent, ends, starts = cut(firsts, rows, cotangent, share + 2 * HALO)
    rounds = [lax.ppermute(array, both, table) for array, table in zip(sent, tables)]
    up = [(i, i + 1) for i in range(seq - 1)]
    down = [(j, i) for i, j in up]
    before = lax.ppermute(ends, "seq", up)
    after = lax.ppermute(starts, "seq", down)
    kept, features = window_forward(
        sides, rounds, first_taps, second_taps, first_matrix, second_matrix
    )

    def shifted(array, step):
        return lax.ppermute(array, "trk", [(i, (i + step) % trk) for i in range(trk)])

    gathered = jnp.concatenate(
        [features, shifted(features, 3), shifted(features, 2), shifted(features, 1)], axis=0
    )
    middle, trunk_output = own_forward(
        limits, before, rows, after, first_taps, second_taps, first_matrix, second_matrix
    )
    gathered, middle = lax.optimization_barrier((gathered, middle))

    partner = [(i, i ^ 1) for i in range(seq)]
    theirs = lax.ppermute(gathered, "seq", partner)
    prediction, their_half, own_half, own, *partials = head(
        turns, gathered, head_weight, pred_cotangent
    )
    their_half = lax.ppermute(their_half, "seq", partner)
    received = [shifted(array, step) for array, step in zip(partials, (1, 2, 3))]

    pieces = outer_products(spots, gathered, theirs, own_half, their_half)
    forth = lax.ppermute(pieces[2, :2], "seq", chip_moves(seq, True, 1))
    back = lax.ppermute(pieces[2, 2:], "seq", chip_moves(seq, True, 3))
    received, pieces = lax.optimization_barrier((received, pieces))

    grad_kept, initial, last = kept_gradient(sides, [own, *received], kept)
    tables = [[(j, i) for i, j in table] for table in tables]
    returned = [
        lax.ppermute(array, both, table)
        for array, table in zip((grad_kept, grad_kept, initial, last), tables)
    ]
    nexts = jnp.concatenate([(widen(pieces[1, :2]) + widen(forth)).astype(BF16), pieces[1, 2:]])
    lasts = jnp.concatenate([pieces[3, :2], (widen(pieces[3, 2:]) + widen(back)).astype(BF16)])
    forth = lax.ppermute(nexts, "seq", chip_moves(seq, True, 1))
    back = lax.ppermute(lasts, "seq", chip_moves(seq, True, 3))
    returned, nexts, lasts = lax.optimization_barrier((returned, nexts, lasts))
    input_gradient = backward(
        limits, returned, before, cotangent, after, middle, rows,
        first_taps, second_taps, first_matrix, second_matrix,
    )
    total = widen(pieces[0]) + widen(forth) + widen(back)
    chunks = total.astype(BF16)
    total = total[0]
    for step in (1, 2, 3):
        total = total + widen(
            lax.ppermute(chunks[step], "seq", chip_moves(seq, False, step))
        )
    rows_each = total.shape[0] // 2
    even, odd = total[:rows_each], total[rows_each:]
    swapped = widen(
        lax.ppermute(jnp.where(core == 0, odd, even).astype(BF16), "seq", partner)
    )
    grad_head = jnp.where(
        core == 0,
        jnp.concatenate([even, swapped], axis=1),
        jnp.concatenate([swapped, odd], axis=1),
    )
    return prediction, trunk_output[None], input_gradient[None], grad_head


def solution(mesh):
    in_specs = (
        P("trk", "seq", None),
        P(),
        P(),
        P(),
        P(),
        P(None, "trk"),
        P(None, "seq", "trk"),
        P("trk", "seq", None),
    )
    out_specs = (
        P(None, "seq", "trk"),
        P("trk", "seq", None),
        P("trk", "seq", None),
        P("seq", "trk"),
    )
    return jax.shard_map(
        on_device, mesh=mesh, in_specs=in_specs, out_specs=out_specs, check_vma=False
    )
```

```python
import jax
import jax.numpy as jnp
from jax import lax
from jax.experimental import pallas as pl
from jax.experimental.pallas import tpu as pltpu
from jax.sharding import PartitionSpec as P

DILATION_FIRST = 4
DILATION_SECOND = 8
HALO = 16
EPSILON = 1e-06
STEP = 16
COLUMNS = 512
SCOPED = 24 << 20

SHARES_BY_ROUND = ((0, 3, 6), (1, 4, 7), (2, 5, 8), (-1, 2, 5))
PIECES = (
    ((2, 64, 80), (0, 0, 112)),
    ((1, 0, 128),),
    ((2, 0, 80), (3, 0, 48)),
    ((0, 0, 128),),
    ((1, 0, 128),),
    ((2, 32, 80), (3, 0, 80)),
    ((0, 0, 128),),
    ((1, 16, 128), (3, 0, 16)),
)


BF16, F32 = jnp.bfloat16, jnp.float32
VMEM = pl.BlockSpec(memory_space=pltpu.VMEM)
SMEM = pl.BlockSpec(memory_space=pltpu.SMEM)


FIRST, SECOND, PLACE, REVERSE, LOW, HIGH, SHIFT, SLOW, FAST, CORE, SEQUENCE = range(11)


def placed(rows, columns, dtype=BF16):
    return pltpu.VMEM((rows, columns), dtype)


def near(array):
    return pltpu.with_memory_space_constraint(array, pltpu.VMEM)


def call(kernel, name, scalars, operands, results, scratch=()):
    return pl.pallas_call(
        kernel,
        out_shape=results,
        in_specs=[SMEM] + [VMEM] * len(operands),
        out_specs=[VMEM] * len(results),
        scratch_shapes=scratch,
        compiler_params=pltpu.CompilerParams(vmem_limit_bytes=SCOPED),
        name=name,
    )(scalars, *operands)


def gelu_and_slope(values):
    k, c = 0.7978845608028654, 0.044715
    square = values * values
    t = jnp.tanh(k * values * (1.0 + c * square))
    half = 0.5 * (1.0 + t)
    slope = half + 0.5 * values * (1.0 - t * t) * (k * (1.0 + 3.0 * c * square))
    return values * half, slope


def inverse_norm(values):
    return lax.rsqrt(jnp.mean(values * values, axis=-1, keepdims=True) + EPSILON)


def span(start, offset=0, size=STEP):
    start = start + offset
    return pl.ds(start if isinstance(start, int) else pl.multiple_of(start, 8), size)


def for_chunks(count, body):
    def store(results):
        for ref, index, value in results:
            ref[index] = value

    def step(k, carry):
        at = pl.multiple_of(k * 2 * STEP, 2 * STEP)
        store(body(at) + body(pl.multiple_of(at + STEP, STEP)))
        return carry

    lax.fori_loop(0, count // 2, step, 0)
    if count % 2:
        store(body((count - 1) * STEP))


def weighted(values_ref, taps_ref, at, offsets):
    base = min(offsets) // 8 * 8
    block = values_ref[span(at, base, 2 * STEP), :]
    total = taps_ref[0:1, :] * block[offsets[0] - base : offsets[0] - base + STEP]
    total += taps_ref[1:2, :] * block[offsets[1] - base : offsets[1] - base + STEP]
    return total + taps_ref[2:3, :] * block[offsets[2] - base : offsets[2] - base + STEP]


def activate(values_ref, out_ref, rows, start=0, inside=None, kept=None):
    def body(at):
        values = values_ref[span(at, start), :]
        inverse = inverse_norm(values)
        result, slope = gelu_and_slope(values * inverse)
        result = result.astype(BF16).astype(F32)
        if inside is not None:
            result = jnp.where(inside(at, result.shape), result, 0.0)
        stores = [(out_ref, (span(at, start), slice(None)), result)]
        if kept is not None:
            stores.append((kept[0], (span(at), slice(None)), slope))
            inverse = jnp.broadcast_to(inverse, (STEP, 128))
            stores.append((kept[1], (span(at), slice(None)), inverse))
        return stores

    for_chunks(rows // STEP, body)


def convolve(values_ref, taps_ref, offsets, out_ref, rows):
    def body(at):
        total = weighted(values_ref, taps_ref, at, offsets).astype(BF16)
        return [(out_ref, (span(at), slice(None)), total)]

    for_chunks(rows // STEP, body)


def product(rows, matrix):
    return jnp.dot(rows, matrix, preferred_element_type=F32)


def product_back(rows, matrix):
    return lax.dot_general(rows, matrix, (((1,), (1,)), ((), ())), preferred_element_type=F32)


def flipped(flag, rows, values):
    row = lax.broadcasted_iota(jnp.int32, (rows, rows), 0)
    column = lax.broadcasted_iota(jnp.int32, (rows, rows), 1)
    target = jnp.where(flag == 1, rows - 1 - row, row)
    return product((column == target).astype(BF16), values).astype(BF16)


def cut_kernel(at_ref, rows_ref, cotangent_ref, one, two, three, four, ends, starts):
    local = rows_ref.shape[0]
    size = one.shape[0]
    one[...] = rows_ref[pl.ds(pl.multiple_of(at_ref[FIRST], 16), size), :]
    two[...] = rows_ref[pl.ds(pl.multiple_of(at_ref[SECOND], 16), size), :]
    three[...] = rows_ref[local - three.shape[0] :, :]
    four[...] = rows_ref[: four.shape[0], :]
    ends[:HALO, :] = rows_ref[local - HALO :, :]
    ends[HALO:, :] = cotangent_ref[local - HALO :, :]
    starts[:HALO, :] = rows_ref[:HALO, :]
    starts[HALO:, :] = cotangent_ref[:HALO, :]


def cut(scalars, rows, cotangent, size):
    sizes = (size, size, 80, 80, 2 * HALO, 2 * HALO)
    results = [placed(n, rows.shape[1]) for n in sizes]
    return call(cut_kernel, "cut", scalars, (rows, cotangent), results)


def window_kernel(
    at_ref, one, two, three, four, taps_ref, taps2_ref, matrix, matrix2,
    slope_ref, features_ref,
    values, active, convolved,
):
    rounds = (one, two, three, four)
    for place, pieces in enumerate(PIECES):

        @pl.when(at_ref[PLACE] == place)
        def _():
            row = 0
            for index, first, last in pieces:
                values[row : row + last - first, :] = rounds[index][first:last, :].astype(F32)
                row += last - first

    size, d = values.shape
    share = size - 2 * HALO
    active[:8, :] = jnp.zeros((8, d), F32)
    active[size + 8 :, :] = jnp.zeros((8, d), F32)
    inner = active.at[8 : size + 8, :]
    activate(values, inner, size)
    q = DILATION_FIRST
    convolve(active, taps_ref, (8 - q, 8, 8 + q), convolved, size)
    for n in range(0, d, COLUMNS):
        part = values[:, n : n + COLUMNS] + product(convolved[...], matrix[:, n : n + COLUMNS])
        values[:, n : n + COLUMNS] = part.astype(BF16).astype(F32)
    activate(values, inner, size)
    q = DILATION_SECOND
    convolve(active, taps2_ref, (8 + HALO - q, 8 + HALO, 8 + HALO + q), convolved, share)
    for n in range(0, d, COLUMNS):
        part = values[HALO : HALO + share, n : n + COLUMNS] + product(
            convolved[:share, :], matrix2[:, n : n + COLUMNS]
        )
        kept = flipped(at_ref[REVERSE], share, part.astype(BF16))
        features, slope = gelu_and_slope(kept.astype(F32))
        slope_ref[:, n : n + COLUMNS] = slope
        features_ref[:, n : n + COLUMNS] = features.astype(BF16)


def window_forward(scalars, rounds, *rest):
    size, d = rounds[0].shape
    share = size - 2 * HALO
    scratch = [pltpu.VMEM((size, d), F32), pltpu.VMEM((size + 16, d), F32), placed(size, d)]
    results = [placed(share, d, F32), placed(share, d)]
    operands = [near(array) for array in (*rounds, *rest)]
    return call(window_kernel, "window_forward", scalars, operands, results, scratch)


def inside_of(at_ref):
    def inside(at, shape):
        row = at + lax.broadcasted_iota(jnp.int32, shape, 0)
        return (row >= at_ref[LOW]) & (row < at_ref[HIGH])

    return inside


def own_kernel(
    at_ref, before, rows_ref, after, taps_ref, taps2_ref, matrix, matrix2,
    middle_ref, result_ref, slope_ref, inverse_ref, slope2_ref, inverse2_ref,
    values, active, convolved,
):
    local, d = rows_ref.shape
    middle = local + 2 * DILATION_SECOND
    edge = HALO - DILATION_SECOND
    values[:HALO, :] = before[:HALO, :].astype(F32)
    values[HALO : HALO + local, :] = rows_ref[...].astype(F32)
    values[HALO + local :, :] = after[:HALO, :].astype(F32)
    activate(values, active, HALO)
    activate(values, active, local, HALO, None, (slope_ref, inverse_ref))
    activate(values, active, HALO, HALO + local)
    q = DILATION_FIRST
    convolve(active, taps_ref, (edge - q, edge, edge + q), convolved, middle)
    for n in range(0, d, COLUMNS):
        part = values[edge : edge + middle, n : n + COLUMNS] + product(
            convolved[...], matrix[:, n : n + COLUMNS]
        )
        part = part.astype(BF16)
        middle_ref[:, n : n + COLUMNS] = part
        values[:middle, n : n + COLUMNS] = part.astype(F32)
    activate(values, active, middle, 0, inside_of(at_ref), (slope2_ref, inverse2_ref))
    q = DILATION_SECOND
    convolve(active, taps2_ref, (0, q, 2 * q), convolved, local)
    for n in range(0, d, COLUMNS):
        part = values[q : q + local, n : n + COLUMNS] + product(
            convolved[:local, :], matrix2[:, n : n + COLUMNS]
        )
        result_ref[:, n : n + COLUMNS] = part.astype(BF16)


def own_forward(scalars, before, rows, after, *rest):
    local, d = rows.shape
    wide, middle = local + 2 * HALO, local + 2 * DILATION_SECOND
    results = [
        placed(middle, d),
        jax.ShapeDtypeStruct((local, d), BF16),
        placed(local, d, F32),
        placed(local, 128, F32),
        placed(middle, d, F32),
        placed(middle, 128, F32),
    ]
    scratch = [pltpu.VMEM((wide, d), F32), pltpu.VMEM((wide, d), F32), placed(middle, d)]
    operands = [near(before), rows, near(after)] + [near(array) for array in rest]
    return call(own_kernel, "own_forward", scalars, operands, results, scratch)


def order_kernel(at_ref, own, one, two, three, out_ref):
    share = own.shape[0]
    for k, piece in enumerate((own, one, two, three)):
        sequence = (at_ref[SEQUENCE] + k) % 4
        out_ref[pl.ds(pl.multiple_of(sequence * share, 16), share), :] = piece[...]


def ordered(scalars, pieces):
    share, d = pieces[0].shape
    operands = [near(array) for array in pieces]
    return call(order_kernel, "order", scalars, operands, [placed(4 * share, d)])[0]


def outer_kernel(
    at_ref, mine_ref, theirs_ref, grad_ref, their_grad_ref, forth_ref, back_ref, rest_ref
):
    step = pl.program_id(0)
    dims = (((0,), (0,)), ((), ()))
    total = lax.dot_general(mine_ref[...], grad_ref[...], dims, preferred_element_type=F32)
    total += lax.dot_general(theirs_ref[...], their_grad_ref[...], dims, preferred_element_type=F32)
    total = total.astype(BF16)
    rows = rest_ref.shape[2]
    relative_x = (step + 4 - at_ref[SLOW]) % 4
    for y in range(4):
        relative_y = (y + 4 - at_ref[FAST]) % 4
        first = jnp.where(at_ref[CORE] == 0, relative_x, relative_y)
        second = jnp.where(at_ref[CORE] == 0, relative_y, relative_x)
        part = total[rows * y : rows * (y + 1)]

        @pl.when((first == 2) & (second < 2))
        def _():
            forth_ref[jnp.minimum(second, 1)] = part

        @pl.when((first == 2) & (second >= 2))
        def _():
            back_ref[jnp.maximum(second, 2) - 2] = part

        @pl.when(first != 2)
        def _():
            rest_ref[jnp.minimum(first, 2), second] = part


def outer_products(scalars, mine, theirs, grad, their_grad):
    bins, d = mine.shape
    tracks = grad.shape[1]
    features = pl.BlockSpec((bins, d // 4), lambda i, at: (0, i))
    whole = pl.BlockSpec((bins, tracks), lambda i, at: (0, 0))
    rows = d // 16
    shapes = ((2, rows, tracks), (2, rows, tracks), (3, 4, rows, tracks))
    return pl.pallas_call(
        outer_kernel,
        out_shape=[pltpu.VMEM(shape, BF16) for shape in shapes],
        grid_spec=pltpu.PrefetchScalarGridSpec(
            num_scalar_prefetch=1,
            grid=(4,),
            in_specs=[features, features, whole, whole],
            out_specs=[
                pl.BlockSpec(shapes[0], lambda i, at: (0, 0, 0)),
                pl.BlockSpec(shapes[1], lambda i, at: (0, 0, 0)),
                pl.BlockSpec(shapes[2], lambda i, at: (0, 0, 0, 0)),
            ],
        ),
        compiler_params=pltpu.CompilerParams(
            dimension_semantics=("arbitrary",), vmem_limit_bytes=SCOPED
        ),
        name="outer_products",
    )(scalars, near(mine), near(theirs), near(grad), near(their_grad))


def ring_kernel(at_ref, rest, forth, back, nexts, lasts):
    nexts[:2] = (rest[1, :2].astype(F32) + forth[...].astype(F32)).astype(BF16)
    nexts[2:] = rest[1, 2:]
    lasts[:2] = rest[2, :2]
    lasts[2:] = (rest[2, 2:].astype(F32) + back[...].astype(F32)).astype(BF16)


def ring_step(scalars, rest, forth, back):
    results = [pltpu.VMEM(rest.shape[1:], BF16)] * 2
    operands = [near(array) for array in (rest, forth, back)]
    return call(ring_kernel, "ring_step", scalars, operands, results)


def turn_kernel(at_ref, rest, forth, back, own, one, two, three):
    for k, out in enumerate((own, one, two, three)):
        total = rest[0, k].astype(F32) + forth[k].astype(F32) + back[k].astype(F32)
        out[...] = total.astype(out.dtype)


def ring_turn(scalars, rest, forth, back):
    rows, tracks = rest.shape[2:]
    results = [placed(rows, tracks, F32)] + [placed(rows, tracks)] * 3
    operands = [near(array) for array in (rest, forth, back)]
    return call(turn_kernel, "ring_turn", scalars, operands, results)


def final_kernel(at_ref, own, one, two, three, kept, sent):
    rows = kept.shape[0]
    for out, core in ((kept, at_ref[CORE]), (sent, 1 - at_ref[CORE])):
        at = pl.ds(pl.multiple_of(core * rows, 16), rows)
        total = own[at, :] + one[at, :].astype(F32) + two[at, :].astype(F32)
        out[...] = (total + three[at, :].astype(F32)).astype(out.dtype)


def ring_final(scalars, pieces):
    rows, tracks = pieces[0].shape
    results = [placed(rows // 2, tracks, F32), placed(rows // 2, tracks)]
    return call(final_kernel, "ring_final", scalars, [near(array) for array in pieces], results)


def kept_kernel(at_ref, own, one, two, three, slope_ref, result_ref, initial_ref, last_ref):
    total = own[...].astype(F32) + one[...].astype(F32)
    total = total + two[...].astype(F32) + three[...].astype(F32)
    share = total.shape[0]
    gradient = flipped(at_ref[REVERSE], share, (slope_ref[...] * total).astype(BF16))
    result_ref[...] = gradient
    initial_ref[...] = gradient[: initial_ref.shape[0]]
    last_ref[...] = gradient[share - last_ref.shape[0] :]


def kept_gradient(scalars, pieces, slope):
    share, d = slope.shape
    results = [placed(share, d), placed(80, d), placed(80, d)]
    operands = [near(array) for array in (*pieces, slope)]
    return call(kept_kernel, "kept_gradient", scalars, operands, results)


def pull_back(values_ref, kept, back_ref, taps_ref, offsets, gradient_ref, shift, write, rows):
    slope_ref, inverse_ref = kept
    d = values_ref.shape[1]

    def body(at):
        inverse = jnp.concatenate([inverse_ref[span(at), :]] * (d // 128), axis=1)
        scaled = values_ref[span(at), :].astype(F32) * inverse
        inner = slope_ref[span(at), :] * weighted(back_ref, taps_ref, at, offsets)
        along = jnp.mean(scaled * inner, axis=-1, keepdims=True)
        total = gradient_ref[span(at, shift), :] + inverse * (inner - scaled * along)
        return write(at, total)

    for_chunks(rows // STEP, body)


def backward_kernel(
    at_ref, one, two, three, four, before, cotangent_ref, after, middle_ref, rows_ref,
    slope_ref, inverse_ref, slope2_ref, inverse2_ref,
    taps_ref, taps2_ref, matrix, matrix2,
    result_ref,
    pool, gradient, wide_gradient, inner_gradient, back,
):
    local, d = rows_ref.shape
    wide = local + 2 * HALO
    middle = local + 2 * DILATION_SECOND
    edge = HALO - DILATION_SECOND
    every = slice(None)
    row = 0
    for piece in (four, one, two, three):
        pool[row : row + piece.shape[0], :] = piece[...]
        row += piece.shape[0]
    wide_gradient[:HALO, :] = before[HALO:, :].astype(F32)
    wide_gradient[HALO : HALO + local, :] = cotangent_ref[...].astype(F32)
    wide_gradient[HALO + local :, :] = after[HALO:, :].astype(F32)

    def place(at):
        come = pool[pl.ds(pl.multiple_of(at_ref[SHIFT] + at, 16), STEP), :].astype(F32)
        total = (come + wide_gradient[span(at), :]).astype(BF16)
        return [
            (gradient, (span(at), every), total),
            (wide_gradient, (span(at), every), total.astype(F32)),
        ]

    for_chunks(wide // STEP, place)
    for n in range(0, d, COLUMNS):
        part = product_back(gradient[...], matrix2[n : n + COLUMNS, :])
        back[:, n : n + COLUMNS] = part.astype(BF16).astype(F32)
    inside = inside_of(at_ref)

    def write_middle(at, total):
        total = jnp.where(inside(at, total.shape), total, 0.0).astype(BF16)
        return [
            (gradient, (span(at), every), total),
            (inner_gradient, (span(at), every), total.astype(F32)),
        ]

    q = DILATION_SECOND
    pull_back(
        middle_ref, (slope2_ref, inverse2_ref), back, taps2_ref, (edge + q, edge, edge - q),
        wide_gradient, edge, write_middle, middle,
    )
    for n in range(0, d, COLUMNS):
        part = product_back(gradient[:middle, :], matrix[n : n + COLUMNS, :])
        back[:middle, n : n + COLUMNS] = part.astype(BF16).astype(F32)

    def write_last(at, total):
        return [(result_ref, (span(at), every), total)]

    edge, q = DILATION_SECOND, DILATION_FIRST
    pull_back(
        rows_ref, (slope_ref, inverse_ref), back, taps_ref, (edge + q, edge, edge - q),
        inner_gradient, edge, write_last, local,
    )


def backward(scalars, rounds, before, cotangent, after, *rest):
    local, d = cotangent.shape
    wide, middle = local + 2 * HALO, local + 2 * DILATION_SECOND
    operands = [near(a) for a in (*rounds, before, cotangent, after, *rest)]
    scratch = [
        placed(2 * 80 + local * 3 // 4, d),
        placed(wide, d),
        pltpu.VMEM((wide, d), F32),
        pltpu.VMEM((middle, d), F32),
        pltpu.VMEM((wide, d), F32),
    ]
    results = [jax.ShapeDtypeStruct((local, d), F32)]
    return call(backward_kernel, "backward", scalars, operands, results, scratch)[0]


def routes(seq, trk, first_block):
    tables = []
    for by_block in SHARES_BY_ROUND:
        table = []
        for block in range(-1, seq * 3 // 8 + 1):
            share = 8 * (block // 3) + by_block[block % 3]
            if not 0 <= share < seq:
                continue
            for z in range(trk):
                target = share if z % 2 == 0 else seq - 1 - share
                table.append(((first_block + block) * trk + z, target * trk + z))
        tables.append(table)
    return tables


def chip_moves(seq, across, step):
    pairs = []
    for i in range(seq):
        x, y, core = i // 8, i // 2 % 4, i % 2
        if (core == 0) == across:
            x = (x + step) % 4
        else:
            y = (y + step) % 4
        pairs.append((i, x * 8 + y * 2 + core))
    return pairs


def on_device(
    inputs,
    first_taps,
    second_taps,
    first_matrix,
    second_matrix,
    head_weight,
    pred_cotangent,
    trunk_cotangent,
):
    seq, trk = lax.axis_size("seq"), lax.axis_size("trk")
    position, z = lax.axis_index("seq"), lax.axis_index("trk")
    reverse = z % 2
    both = ("seq", "trk")
    rows, cotangent = inputs[0], trunk_cotangent[0]
    local = rows.shape[0]
    share = local * 3 // 8
    first_block = 5 * seq // 16
    tables = routes(seq, trk, first_block)
    phase = (position + 3 * seq - first_block) % 3
    last_phase = phase // 2
    core = position % 2
    edge = DILATION_SECOND
    scalars = jnp.stack(
        [
            16 * (phase + last_phase),
            80 + 32 * phase - 16 * last_phase,
            jnp.where(reverse == 1, seq - 1 - position, position) % 8,
            reverse,
            jnp.where(position == 0, edge, 0),
            jnp.where(position == seq - 1, edge + local, local + 2 * edge),
            64 - 32 * phase,
            position // 8,
            position // 2 % 4,
            core,
            z,
        ]
    ).astype(jnp.int32)
    weights = [near(a) for a in (first_taps, second_taps, first_matrix, second_matrix)]

    *sent, ends, starts = cut(scalars, rows, cotangent, share + 2 * HALO)
    rounds = [lax.ppermute(array, both, table) for array, table in zip(sent, tables)]
    up = [(i, i + 1) for i in range(seq - 1)]
    down = [(j, i) for i, j in up]
    before = lax.ppermute(ends, "seq", up)
    after = lax.ppermute(starts, "seq", down)
    middle, trunk_output, *kept = own_forward(scalars, before, rows, after, *weights)
    rounds, middle = lax.optimization_barrier((rounds, middle))
    slope, features = window_forward(scalars, rounds, *weights)

    def shifted(array, step):
        return lax.ppermute(array, "trk", [(i, (i + step) % trk) for i in range(trk)])

    gathered = ordered(
        scalars, [features, shifted(features, 3), shifted(features, 2), shifted(features, 1)]
    )
    partner = [(i, i ^ 1) for i in range(seq)]
    theirs = lax.ppermute(gathered, "seq", partner)
    logits = product(gathered, head_weight)
    prediction = jax.nn.softplus(logits).astype(BF16)
    flat_cotangent = pred_cotangent.reshape(-1, pred_cotangent.shape[-1])
    grad_logit = (flat_cotangent.astype(F32) * jax.nn.sigmoid(logits)).astype(BF16)
    partials = product_back(grad_logit, head_weight).astype(BF16)

    def partial_of(step):
        return lax.dynamic_slice_in_dim(partials, (z + step) % trk * share, share, 0)

    received = [shifted(partial_of(step), step) for step in (1, 2, 3)]

    tracks = grad_logit.shape[1] // 2
    halves = grad_logit[:, :tracks], grad_logit[:, tracks:]
    own_half = jnp.where(core == 0, halves[0], halves[1])
    their_half = lax.ppermute(jnp.where(core == 0, halves[1], halves[0]), "seq", partner)
    forth, back, rest = outer_products(scalars, gathered, theirs, own_half, their_half)
    forth = lax.ppermute(forth, "seq", chip_moves(seq, True, 1))
    back = lax.ppermute(back, "seq", chip_moves(seq, True, 3))
    received, rest = lax.optimization_barrier((received, rest))

    grad_kept, initial, last = kept_gradient(scalars, [partial_of(0), *received], slope)
    tables = [[(j, i) for i, j in table] for table in tables]
    returned = [
        lax.ppermute(array, both, table)
        for array, table in zip((grad_kept, grad_kept, initial, last), tables)
    ]
    forth, back, grad_kept = lax.optimization_barrier((forth, back, grad_kept))
    nexts, lasts = ring_step(scalars, rest, forth, back)
    forth = lax.ppermute(nexts, "seq", chip_moves(seq, True, 1))
    back = lax.ppermute(lasts, "seq", chip_moves(seq, True, 3))
    returned, nexts, lasts = lax.optimization_barrier((returned, nexts, lasts))
    input_gradient = backward(
        scalars, returned, before, cotangent, after, middle, rows, *kept, *weights
    )
    total, *chunks = ring_turn(scalars, rest, forth, back)
    chunks = [
        lax.ppermute(chunk, "seq", chip_moves(seq, False, step))
        for chunk, step in zip(chunks, (1, 2, 3))
    ]
    mine, sent = ring_final(scalars, [total, *chunks])
    swapped = lax.ppermute(sent, "seq", partner).astype(F32)
    grad_head = jnp.where(
        core == 0,
        jnp.concatenate([mine, swapped], axis=1),
        jnp.concatenate([swapped, mine], axis=1),
    )
    return (
        prediction.reshape(pred_cotangent.shape),
        trunk_output[None],
        input_gradient[None],
        grad_head,
    )


def solution(mesh):
    in_specs = (
        P("trk", "seq", None),
        P(),
        P(),
        P(),
        P(),
        P(None, "trk"),
        P(None, "seq", "trk"),
        P("trk", "seq", None),
    )
    out_specs = (
        P(None, "seq", "trk"),
        P("trk", "seq", None),
        P("trk", "seq", None),
        P("seq", "trk"),
    )
    return jax.shard_map(
        on_device, mesh=mesh, in_specs=in_specs, out_specs=out_specs, check_vma=False
    )
```
